128 devices in a mesh: row: 8 (over y_lo, z), col: 16 (over x, y_hi, core).
Axes of the slice: x: 4, y: 4 (y_hi: 2, y_lo: 2; y = y_hi * 2 + y_lo), z: 4, core: 2. Of those that a mesh axis runs over, the one named last changes fastest.
Arguments:
- feats_one: bfloat16 [65536, 256], P(('row', 'col')), may hold values from -6 to 6
- feats_two: bfloat16 [65536, 256], P(('row', 'col')), may hold values from -6 to 6
- target_view: bfloat16 [65536, 256], P(('row', 'col')), may hold values from -6 to 6
- negatives: int32 [65536], P(('row', 'col')), may hold values from 0 to 511
- weight_one: bfloat16 [256, 256], replicated, may hold values from -0.375 to 0.375
- weight_two: bfloat16 [256, 256], replicated, may hold values from -0.375 to 0.375
- block_tiles: bfloat16 [81920, 128, 128], P(('row', 'col')), may hold values from -0.15625 to 0.15625
- tile_rows: int32 [81920], P(('row', 'col')), may hold values from 0 to 31
- tile_cols: int32 [81920], P(('row', 'col')), may hold values from 0 to 31
- block_counts: int32 [128], P(('row', 'col')), may hold values from 80 to 640, as said below
- need_rows: int32 [128, 16, 2], P(('row', 'col')), may hold values from 0 to 3, as said below
Outputs:
- grad_hidden: bfloat16 [65536, 256], P(('row', 'col'))
- grad_first: float32 [256, 256], replicated
- grad_second: float32 [256, 256], replicated
The draws below stay inside these ranges and needn't reach their ends.
Inputs may be any that keep to these rules, and one draw needn't show every extreme that they name: `need_rows`: for each owner and source, the 2 entries are distinct. `block_counts`: live tiles of one block list.
All inputs are finite; a program needn't handle non-finite values.
Results may differ from the reference program's by a relative error of at most 0.0063.
Values may be sent and summed in bfloat16 or wider, within the bound.
No kernel may reach another device: no remote copies, remote signals or barrier semaphores. Data moves between devices by JAX's collectives and lax.ppermute only.
A program may use at most 192 MiB of HBM per device.

```python
import math
import jax
import jax.numpy as jnp
from jax import lax

F = 256
TILE = 128
BLOCK_DEG = 160
NT_DEV = 4
NODE_DEV = 512
SLOT = 2
CAP = 640
SOURCES = 16
OWNERS = 128
ROW_SLOTS = 32
COL_TILES = 32
NODES = 65536
N_COL = 16


def draw_block_counts(key, part):
    lighter = jax.random.randint(jax.random.fold_in(key, 11), (OWNERS,), CAP // 8, CAP // 2 + 1)
    heaviest = jax.random.randint(jax.random.fold_in(key, 12), (), 0, OWNERS)
    return jnp.where(jnp.arange(OWNERS) == heaviest, CAP, lighter).astype(jnp.int32)


def draw_need_rows(key, part):
    subkeys = jax.random.split(jax.random.fold_in(key, 21), OWNERS * SOURCES)

    def one_list(subkey):
        return jax.random.permutation(subkey, NT_DEV)
    orders = jax.vmap(one_list)(subkeys)
    return orders[:, :SLOT].reshape(OWNERS, SOURCES, SLOT).astype(jnp.int32)


def plant(values, stream_key, least, largest):
    dims = values.shape
    index_at = [jax.random.randint(jax.random.fold_in(stream_key, axis), (), 0, dims[axis]) for axis in range(len(dims))]
    values = values.at[tuple(index_at)].set(least)
    longest = dims.index(max(dims))
    index_at[longest] = (index_at[longest] + 1) % dims[longest]
    return values.at[tuple(index_at)].set(largest)


def shard_levels(rng, extent, cuts, low, largest):
    def one(axis_at, parts):
        heights = jax.random.uniform(jax.random.fold_in(jax.random.fold_in(rng, 6), axis_at), (parts,), jnp.float32, low / len(cuts), largest / len(cuts))
        return jnp.repeat(jnp.exp(heights), extent[axis_at] // parts).reshape((-1,) + (1,) * (len(extent) - axis_at - 1))

    gain = one(*cuts[0])
    for cut in cuts[1:]:
        gain = gain * one(*cut)
    return gain


def noise(key, extent, width, most, cuts=(), kind=jnp.bfloat16):
    array = jax.random.normal(key, extent, jnp.float32) * width
    if len(cuts) > 0:
        array = shard_levels(key, extent, cuts, -0.22, 0.18) * array
    return jnp.clip(array, min=-most, max=most).astype(kind)


def setup_inputs(seed: int = 0) -> dict:
    key_list = jax.random.split(jax.random.key(seed), 12)
    return {
        "feats_one": noise(key_list[0], (NODES, F), 1.0, 6.0, ((0, 128),)),
        "feats_two": noise(key_list[1], (NODES, F), 1.0, 6.0, ((0, 128),)),
        "target_view": noise(key_list[2], (NODES, F), 1.0, 6.0, ((0, 128),)),
        "negatives": plant(jax.random.randint(key_list[3], (NODES,), 0, NODE_DEV), jax.random.fold_in(key_list[3], 1), 0, NODE_DEV - 1).astype(jnp.int32),
        "weight_one": noise(key_list[4], (F, F), F ** -0.5, 0.375),
        "weight_two": noise(key_list[5], (F, F), F ** -0.5, 0.375),
        "block_tiles": noise(key_list[6], (OWNERS * CAP, TILE, TILE), (TILE * BLOCK_DEG // 16) ** -0.5, 0.15625, ((0, 128),)),
        "tile_rows": plant(jax.random.randint(key_list[7], (OWNERS * CAP,), 0, ROW_SLOTS), jax.random.fold_in(key_list[7], 1), 0, ROW_SLOTS - 1).astype(jnp.int32),
        "tile_cols": plant(jax.random.randint(key_list[8], (OWNERS * CAP,), 0, COL_TILES), jax.random.fold_in(key_list[8], 1), 0, COL_TILES - 1).astype(jnp.int32),
        "block_counts": draw_block_counts(jax.random.fold_in(key_list[11], 71), 0),
        "need_rows": draw_need_rows(jax.random.fold_in(key_list[11], 71), 0),
    }


def silu_slope(values):
    sig = jax.nn.sigmoid(values)
    return sig * (1.0 + values * (1.0 - sig))

def reference(feats_one, feats_two, target_view, negatives, weight_one, weight_two, block_tiles, tile_rows, tile_cols, block_counts, need_rows):
    node_total = feats_two.shape[0]
    inverse_root = 1.0 / math.sqrt(F)
    pre_two = jnp.dot(feats_two, weight_two, preferred_element_type=jnp.float32)
    hidden = jax.nn.silu(pre_two)
    offsets = jnp.arange(node_total, dtype=jnp.int32) // NODE_DEV * NODE_DEV
    partner = offsets + negatives
    partner_rows = hidden[partner]
    target_full = target_view.astype(jnp.float32)
    s_pos = lax.optimization_barrier(jnp.sum(hidden * target_full, axis=-1)) * inverse_root
    s_neg = lax.optimization_barrier(jnp.sum(hidden * partner_rows, axis=-1)) * inverse_root
    prob_pos = jax.nn.sigmoid(-s_pos)
    prob_neg = jax.nn.sigmoid(s_neg)
    grad_out = -prob_pos[:, None] * target_full + prob_neg[:, None] * partner_rows
    grad_out = grad_out + jax.ops.segment_sum(prob_neg[:, None] * hidden, partner, num_segments=node_total)
    dpre_two = (grad_out * silu_slope(pre_two)).astype(jnp.bfloat16)
    grad_second = jnp.dot(feats_two.T, dpre_two, preferred_element_type=jnp.float32) * (1.0 / math.sqrt(NODES))
    message = jnp.dot(dpre_two, weight_two.T, preferred_element_type=jnp.float32).astype(jnp.bfloat16)
    entries = OWNERS * CAP
    entry_ids = jnp.arange(entries, dtype=jnp.int32)
    owner = entry_ids // CAP
    live = (entry_ids % CAP < block_counts[owner]).astype(jnp.float32)
    row_index = owner // N_COL
    col_index = owner % N_COL
    source = tile_rows // SLOT
    position = tile_rows % SLOT
    need_flat = need_rows.reshape(-1)
    local_tile = need_flat[(owner * SOURCES + source) * SLOT + position]
    row_tile = (row_index * N_COL + source) * NT_DEV + local_tile
    col_tile = (tile_cols // NT_DEV * N_COL + col_index) * NT_DEV + tile_cols % NT_DEV
    message_tiles = message.reshape(-1, TILE, F)
    block_len = 256 if entries % 256 == 0 else entries
    rounds = entries // block_len

    def add_block(summed_tiles, pieces):
        tile_part, row_part, col_part, live_part = pieces
        gathered = message_tiles[row_part].astype(jnp.float32)
        contrib = jnp.einsum('ktu,ktf->kuf', tile_part.astype(jnp.float32), gathered)
        contrib = contrib * live_part[:, None, None]
        return (summed_tiles + jax.ops.segment_sum(contrib, col_part, num_segments=node_total // TILE), None)
    start_tiles = jnp.zeros((node_total // TILE, TILE, F), jnp.float32)
    summed_tiles, _ = lax.scan(add_block, start_tiles, (block_tiles.reshape(rounds, block_len, TILE, TILE), row_tile.reshape(rounds, block_len), col_tile.reshape(rounds, block_len), live.reshape(rounds, block_len)))
    grad_hidden = summed_tiles.reshape(node_total, F).astype(jnp.bfloat16)
    pre_one = jnp.dot(feats_one, weight_one, preferred_element_type=jnp.float32)
    dpre_one = (grad_hidden.astype(jnp.float32) * silu_slope(pre_one)).astype(jnp.bfloat16)
    grad_first = jnp.dot(feats_one.T, dpre_one, preferred_element_type=jnp.float32) * (1.0 / math.sqrt(NODES))
    return (grad_hidden, grad_first, grad_second)
```

```python
import math

import jax
import jax.numpy as jnp
from jax import lax
from jax.experimental import pallas as pl
from jax.experimental.pallas import tpu as pltpu
from jax.sharding import PartitionSpec as P

F32 = jnp.float32
BF16 = jnp.bfloat16
CHUNK = 16
RING = 4


def sigmoid(values):
    return jax.nn.sigmoid(values)


def dot(left, right, left_dim, right_dim):
    return lax.dot_general(
        left, right, (((left_dim,), (right_dim,)), ((), ())), preferred_element_type=F32
    )


def split(values):
    high = values.astype(BF16)
    low = (values - high.astype(F32)).astype(BF16)
    return jnp.concatenate([high, low], axis=1)


def message_kernel(
    need_ref, feats_ref, target_ref, negatives_ref, weight_ref, send_ref, grad_ref, message_ref
):
    nodes, features = feats_ref.shape
    tiles, tile_size, _ = message_ref.shape
    inverse_root = 1.0 / math.sqrt(features)
    feats = feats_ref[...]
    weight = weight_ref[...]
    pre = dot(feats, weight, 1, 0)
    sig = sigmoid(pre)
    hidden = pre * sig
    ids = lax.broadcasted_iota(jnp.int32, (nodes, nodes), 0)
    picks = jnp.where(ids == negatives_ref[...], 1.0, 0.0).astype(BF16)
    both = dot(picks, split(hidden), 0, 0)
    partner = both[:, :features] + both[:, features:]
    target = target_ref[...].astype(F32)
    s_pos = jnp.sum(hidden * target, axis=-1, keepdims=True) * inverse_root
    s_neg = jnp.sum(hidden * partner, axis=-1, keepdims=True) * inverse_root
    prob_pos = sigmoid(-s_pos)
    prob_neg = sigmoid(s_neg)
    both = dot(picks, split(prob_neg * hidden), 1, 0)
    grad_out = prob_neg * partner - prob_pos * target + both[:, :features] + both[:, features:]
    dpre = (grad_out * (sig * (1.0 + pre * (1.0 - sig)))).astype(BF16)
    message = dot(dpre, weight, 1, 1).astype(BF16)
    message_ref[...] = message.reshape(tiles, tile_size, features)
    grad_ref[...] = dot(feats, dpre, 0, 0)

    for slot in range(send_ref.shape[0]):
        send_ref[slot] = message_ref[need_ref[slot]]


def product_kernel(
    rows_ref, cols_ref, count_ref, tiles_ref, received_ref, out_ref, sums_ref, buffer_ref, sems
):
    col_tiles = out_ref.shape[0]
    count = count_ref[0]
    chunks = (count + CHUNK - 1) // CHUNK

    def fetch(chunk):
        slot = lax.rem(chunk, RING)
        return pltpu.make_async_copy(
            tiles_ref.at[pl.ds(chunk * CHUNK, CHUNK)], buffer_ref.at[slot], sems.at[slot]
        )

    for ahead in range(RING - 1):

        @pl.when(ahead < chunks)
        def _():
            fetch(jnp.int32(ahead)).start()

    sums_ref[...] = jnp.zeros(sums_ref.shape, F32)

    def step(chunk, carry):
        @pl.when(chunk + RING - 1 < chunks)
        def _():
            fetch(chunk + RING - 1).start()

        fetch(chunk).wait()
        slot = lax.rem(chunk, RING)
        for at in range(CHUNK):
            k = chunk * CHUNK + at
            col = jnp.where(k < count, cols_ref[k], col_tiles)
            part = dot(buffer_ref[slot, at], received_ref[rows_ref[k]], 0, 0)
            sums_ref[col] += part
        return carry

    lax.fori_loop(0, chunks, step, 0)
    out_ref[...] = sums_ref[:col_tiles].astype(BF16)


def finish_kernel(parts_ref, feats_ref, weight_ref, second_ref, hidden_ref, send_ref):
    sources = parts_ref.shape[0]
    total = parts_ref[0].astype(F32)
    for source in range(1, sources):
        total = total + parts_ref[source].astype(F32)
    grad_hidden = total.astype(BF16)
    hidden_ref[...] = grad_hidden
    feats = feats_ref[...]
    pre = dot(feats, weight_ref[...], 1, 0)
    sig = sigmoid(pre)
    slope = sig * (1.0 + pre * (1.0 - sig))
    dpre = (grad_hidden.astype(F32) * slope).astype(BF16)
    first = dot(feats, dpre, 0, 0)
    features = first.shape[0]
    lanes = send_ref.shape[2]
    halves = features // lanes
    block = send_ref.shape[1]
    per_grad = features // block * halves
    for which, grad in enumerate((first, second_ref[...])):
        for half in range(halves):
            piece = grad[:, half * lanes : (half + 1) * lanes].astype(BF16)
            piece = piece.reshape(features // block, block, lanes)
            for row in range(features // block):
                send_ref[which * per_grad + row * halves + half] = piece[row]


def on_device(
    feats_one,
    feats_two,
    target_view,
    negatives,
    weight_one,
    weight_two,
    block_tiles,
    tile_rows,
    tile_cols,
    block_counts,
    need_rows,
):
    node_dev, features = feats_two.shape
    tile_size = block_tiles.shape[1]
    sources = lax.axis_size("col")
    row_group = lax.axis_size("row")
    devices = sources * row_group
    tiles_dev = node_dev // tile_size
    slot_count = need_rows.shape[2]
    col_count = row_group * tiles_dev
    row_slots = sources * slot_count
    weight_norm = 1.0 / math.sqrt(node_dev * devices)
    vmem = pl.BlockSpec(memory_space=pltpu.VMEM)
    smem = pl.BlockSpec(memory_space=pltpu.SMEM)

    wanted = lax.all_to_all(need_rows[0], "col", 0, 0, tiled=True)
    send, second = pl.pallas_call(
        message_kernel,
        out_shape=(
            jax.ShapeDtypeStruct((row_slots, tile_size, features), BF16),
            jax.ShapeDtypeStruct((features, features), F32),
        ),
        in_specs=[smem, vmem, vmem, vmem, vmem],
        out_specs=(vmem, vmem),
        scratch_shapes=[pltpu.VMEM((tiles_dev, tile_size, features), BF16)],
        name="message",
    )(wanted.reshape(row_slots), feats_two, target_view, negatives.reshape(1, node_dev), weight_two)
    received = lax.all_to_all(
        send.reshape(sources, slot_count * tile_size, features), "col", 0, 0, tiled=True
    ).reshape(row_slots, tile_size, features)
    partial = pl.pallas_call(
        product_kernel,
        out_shape=jax.ShapeDtypeStruct((col_count, tile_size, features), BF16),
        in_specs=[smem, smem, smem, pl.BlockSpec(memory_space=pl.ANY), vmem],
        out_specs=vmem,
        scratch_shapes=[
            pltpu.VMEM((col_count + 1, tile_size, features), F32),
            pltpu.VMEM((RING, CHUNK, tile_size, tile_size), BF16),
            pltpu.SemaphoreType.DMA((RING,)),
        ],
        name="product",
    )(tile_rows, tile_cols, block_counts, block_tiles, received)
    parts = lax.all_to_all(
        partial.reshape(row_group, node_dev, features), "row", 0, 0, tiled=True
    )
    lanes = 128
    block = 2 * features * features // (devices * lanes)
    grad_hidden, grads = pl.pallas_call(
        finish_kernel,
        out_shape=(
            jax.ShapeDtypeStruct((node_dev, features), BF16),
            jax.ShapeDtypeStruct((devices, block, lanes), BF16),
        ),
        in_specs=[vmem] * 4,
        out_specs=(vmem, vmem),
        name="finish",
    )(parts, feats_one, weight_one, second)
    pieces = lax.all_to_all(grads, ("row", "col"), 0, 0, tiled=True)
    mine = jnp.sum(pieces.astype(F32), axis=0, keepdims=True) * weight_norm
    whole = lax.all_to_all(
        jnp.broadcast_to(mine, (devices, block, lanes)), ("row", "col"), 0, 0, tiled=True
    )
    whole = whole.reshape(2, features // block, features // lanes, block, lanes)
    whole = whole.transpose(0, 1, 3, 2, 4).reshape(2, features, features)
    return (grad_hidden, whole[0], whole[1])


def solution(mesh):
    return jax.shard_map(
        on_device,
        mesh=mesh,
        in_specs=(
            P(("row", "col"), None),
            P(("row", "col"), None),
            P(("row", "col"), None),
            P(("row", "col")),
            P(),
            P(),
            P(("row", "col"), None, None),
            P(("row", "col")),
            P(("row", "col")),
            P(("row", "col")),
            P(("row", "col"), None, None),
        ),
        out_specs=(P(("row", "col"), None), P(), P()),
        check_vma=False,
    )
```

```python
import math

import jax
import jax.numpy as jnp
from jax import lax
from jax.experimental import pallas as pl
from jax.experimental.pallas import tpu as pltpu
from jax.sharding import PartitionSpec as P

F32 = jnp.float32
BF16 = jnp.bfloat16
CHUNK = 16
RING = 4


def sigmoid(values):
    return jax.nn.sigmoid(values)


def dot(left, right, left_dim, right_dim):
    return lax.dot_general(
        left, right, (((left_dim,), (right_dim,)), ((), ())), preferred_element_type=F32
    )


def split(values):
    high = values.astype(BF16)
    low = (values - high.astype(F32)).astype(BF16)
    return jnp.concatenate([high, low], axis=1)


def message_kernel(
    feats_ref, target_ref, negatives_ref, weight_ref, message_ref, grad_ref
):
    nodes, features = feats_ref.shape
    tiles, _, tile_size = message_ref.shape
    inverse_root = 1.0 / math.sqrt(features)
    feats = feats_ref[...]
    weight = weight_ref[...]
    pre = dot(feats, weight, 1, 0)
    sig = sigmoid(pre)
    hidden = pre * sig
    ids = lax.broadcasted_iota(jnp.int32, (nodes, nodes), 0)
    picks = jnp.where(ids == negatives_ref[...], 1.0, 0.0).astype(BF16)
    both = dot(picks, split(hidden), 0, 0)
    partner = both[:, :features] + both[:, features:]
    target = target_ref[...].astype(F32)
    s_pos = jnp.sum(hidden * target, axis=-1, keepdims=True) * inverse_root
    s_neg = jnp.sum(hidden * partner, axis=-1, keepdims=True) * inverse_root
    prob_pos = sigmoid(-s_pos)
    prob_neg = sigmoid(s_neg)
    both = dot(picks, split(prob_neg * hidden), 1, 0)
    grad_out = prob_neg * partner - prob_pos * target + both[:, :features] + both[:, features:]
    dpre = (grad_out * (sig * (1.0 + pre * (1.0 - sig)))).astype(BF16)
    message = dot(weight, dpre, 1, 1).astype(BF16)
    for tile in range(tiles):
        message_ref[tile] = message[:, tile * tile_size : (tile + 1) * tile_size]
    grad_ref[...] = dot(feats, dpre, 0, 0)


def select_kernel(need_ref, message_ref, send_ref):
    for slot in range(send_ref.shape[0]):
        send_ref[slot] = message_ref[need_ref[slot]]


def product_kernel(
    rows_ref, cols_ref, count_ref, tiles_ref, received_ref, out_ref, sums_ref, buffer_ref, sems
):
    col_tiles = out_ref.shape[0]
    count = count_ref[0]
    chunks = (count + CHUNK - 1) // CHUNK

    def fetch(chunk):
        slot = lax.rem(chunk, RING)
        return pltpu.make_async_copy(
            tiles_ref.at[pl.ds(chunk * CHUNK, CHUNK)], buffer_ref.at[slot], sems.at[slot]
        )

    for ahead in range(RING - 1):

        @pl.when(ahead < chunks)
        def _():
            fetch(jnp.int32(ahead)).start()

    sums_ref[...] = jnp.zeros(sums_ref.shape, F32)

    def step(chunk, carry):
        @pl.when(chunk + RING - 1 < chunks)
        def _():
            fetch(chunk + RING - 1).start()

        fetch(chunk).wait()
        slot = lax.rem(chunk, RING)
        for at in range(CHUNK):
            k = chunk * CHUNK + at
            col = jnp.where(k < count, cols_ref[k], col_tiles)
            part = dot(received_ref[rows_ref[k]], buffer_ref[slot, at], 1, 0)
            sums_ref[col] += part
        return carry

    lax.fori_loop(0, chunks, step, 0)
    out_ref[...] = sums_ref[:col_tiles].astype(BF16)


def finish_kernel(parts_ref, feats_ref, weight_ref, second_ref, hidden_ref, send_ref):
    sources = parts_ref.shape[0]
    total = parts_ref[0].astype(F32)
    for source in range(1, sources):
        total = total + parts_ref[source].astype(F32)
    grad_hidden = jnp.concatenate(
        [total[tile].T for tile in range(total.shape[0])], axis=0
    ).astype(BF16)
    hidden_ref[...] = grad_hidden
    feats = feats_ref[...]
    pre = dot(feats, weight_ref[...], 1, 0)
    sig = sigmoid(pre)
    slope = sig * (1.0 + pre * (1.0 - sig))
    dpre = (grad_hidden.astype(F32) * slope).astype(BF16)
    first = dot(feats, dpre, 0, 0)
    features = first.shape[0]
    lanes = send_ref.shape[2]
    halves = features // lanes
    block = send_ref.shape[1]
    per_grad = features // block * halves
    for which, grad in enumerate((first, second_ref[...])):
        for half in range(halves):
            piece = grad[:, half * lanes : (half + 1) * lanes].astype(BF16)
            piece = piece.reshape(features // block, block, lanes)
            for row in range(features // block):
                send_ref[which * per_grad + row * halves + half] = piece[row]


def on_device(
    feats_one,
    feats_two,
    target_view,
    negatives,
    weight_one,
    weight_two,
    block_tiles,
    tile_rows,
    tile_cols,
    block_counts,
    need_rows,
):
    node_dev, features = feats_two.shape
    tile_size = block_tiles.shape[1]
    sources = lax.axis_size("col")
    row_group = lax.axis_size("row")
    devices = sources * row_group
    tiles_dev = node_dev // tile_size
    slot_count = need_rows.shape[2]
    col_count = row_group * tiles_dev
    row_slots = sources * slot_count
    weight_norm = 1.0 / math.sqrt(node_dev * devices)
    vmem = pl.BlockSpec(memory_space=pltpu.VMEM)
    smem = pl.BlockSpec(memory_space=pltpu.SMEM)

    wanted = lax.all_to_all(need_rows[0], "col", 0, 0, tiled=True)
    message, second = pl.pallas_call(
        message_kernel,
        out_shape=(
            jax.ShapeDtypeStruct((tiles_dev, features, tile_size), BF16),
            jax.ShapeDtypeStruct((features, features), F32),
        ),
        in_specs=[vmem] * 4,
        out_specs=(vmem, vmem),
        name="message",
    )(feats_two, target_view, negatives.reshape(1, node_dev), weight_two)
    send = pl.pallas_call(
        select_kernel,
        out_shape=jax.ShapeDtypeStruct((row_slots, features, tile_size), BF16),
        in_specs=[smem, vmem],
        out_specs=vmem,
        name="select",
    )(wanted.reshape(row_slots), message)
    received = lax.all_to_all(
        send.reshape(sources, slot_count * features, tile_size), "col", 0, 0, tiled=True
    ).reshape(row_slots, features, tile_size)
    partial = pl.pallas_call(
        product_kernel,
        out_shape=jax.ShapeDtypeStruct((col_count, features, tile_size), BF16),
        in_specs=[smem, smem, smem, pl.BlockSpec(memory_space=pl.ANY), vmem],
        out_specs=vmem,
        scratch_shapes=[
            pltpu.VMEM((col_count + 1, features, tile_size), F32),
            pltpu.VMEM((RING, CHUNK, tile_size, tile_size), BF16),
            pltpu.SemaphoreType.DMA((RING,)),
        ],
        name="product",
    )(tile_rows, tile_cols, block_counts, block_tiles, received)
    parts = lax.all_to_all(
        partial.reshape(row_group, tiles_dev * features, tile_size), "row", 0, 0, tiled=True
    ).reshape(row_group, tiles_dev, features, tile_size)
    lanes = 128
    block = 2 * features * features // (devices * lanes)
    grad_hidden, grads = pl.pallas_call(
        finish_kernel,
        out_shape=(
            jax.ShapeDtypeStruct((node_dev, features), BF16),
            jax.ShapeDtypeStruct((devices, block, lanes), BF16),
        ),
        in_specs=[vmem] * 4,
        out_specs=(vmem, vmem),
        name="finish",
    )(parts, feats_one, weight_one, second)
    pieces = lax.all_to_all(grads, ("row", "col"), 0, 0, tiled=True)
    mine = jnp.sum(pieces.astype(F32), axis=0, keepdims=True) * weight_norm
    whole = lax.all_to_all(
        jnp.broadcast_to(mine, (devices, block, lanes)), ("row", "col"), 0, 0, tiled=True
    )
    whole = whole.reshape(2, features // block, features // lanes, block, lanes)
    whole = whole.transpose(0, 1, 3, 2, 4).reshape(2, features, features)
    return (grad_hidden, whole[0], whole[1])


def solution(mesh):
    return jax.shard_map(
        on_device,
        mesh=mesh,
        in_specs=(
            P(("row", "col"), None),
            P(("row", "col"), None),
            P(("row", "col"), None),
            P(("row", "col")),
            P(),
            P(),
            P(("row", "col"), None, None),
            P(("row", "col")),
            P(("row", "col")),
            P(("row", "col")),
            P(("row", "col"), None, None),
        ),
        out_specs=(P(("row", "col"), None), P(), P()),
        check_vma=False,
    )
```

```python
import math

import jax
import jax.numpy as jnp
from jax import lax
from jax.experimental import pallas as pl
from jax.experimental.pallas import tpu as pltpu
from jax.sharding import PartitionSpec as P

F32 = jnp.float32
BF16 = jnp.bfloat16
CHUNK = 16
RING = 4


def sigmoid(values):
    return jax.nn.sigmoid(values)


def dot(left, right, left_dim, right_dim):
    return lax.dot_general(
        left, right, (((left_dim,), (right_dim,)), ((), ())), preferred_element_type=F32
    )


def split(values):
    high = values.astype(BF16)
    low = (values - high.astype(F32)).astype(BF16)
    return jnp.concatenate([high, low], axis=1)


def message_kernel(
    feats_ref, target_ref, negatives_ref, weight_ref, message_ref, grad_ref
):
    nodes, features = feats_ref.shape
    tiles, _, tile_size = message_ref.shape
    inverse_root = 1.0 / math.sqrt(features)
    feats = feats_ref[...]
    weight = weight_ref[...]
    pre = dot(feats, weight, 1, 0)
    sig = sigmoid(pre)
    hidden = pre * sig
    ids = lax.broadcasted_iota(jnp.int32, (nodes, nodes), 0)
    picks = jnp.where(ids == negatives_ref[...], 1.0, 0.0).astype(BF16)
    both = dot(picks, split(hidden), 0, 0)
    partner = both[:, :features] + both[:, features:]
    target = target_ref[...].astype(F32)
    s_pos = jnp.sum(hidden * target, axis=-1, keepdims=True) * inverse_root
    s_neg = jnp.sum(hidden * partner, axis=-1, keepdims=True) * inverse_root
    prob_pos = sigmoid(-s_pos)
    prob_neg = sigmoid(s_neg)
    both = dot(picks, split(prob_neg * hidden), 1, 0)
    grad_out = prob_neg * partner - prob_pos * target + both[:, :features] + both[:, features:]
    dpre = (grad_out * (sig * (1.0 + pre * (1.0 - sig)))).astype(BF16)
    message = dot(weight, dpre, 1, 1).astype(BF16)
    for tile in range(tiles):
        message_ref[tile] = message[:, tile * tile_size : (tile + 1) * tile_size]
    grad_ref[...] = dot(feats, dpre, 0, 0)


def select_kernel(need_ref, message_ref, send_ref):
    slots = need_ref.shape[1]
    for slot in range(send_ref.shape[0]):
        send_ref[slot] = message_ref[need_ref[slot // slots, slot % slots]]


def product_kernel(
    rows_ref, cols_ref, count_ref, tiles_ref, received_ref, out_ref, sums_ref, buffer_ref, sems
):
    col_tiles = out_ref.shape[0]
    count = count_ref[0]
    chunks = (count + CHUNK - 1) // CHUNK

    def fetch(chunk):
        slot = lax.rem(chunk, RING)
        return pltpu.make_async_copy(
            tiles_ref.at[pl.ds(chunk * CHUNK, CHUNK)], buffer_ref.at[slot], sems.at[slot]
        )

    for ahead in range(RING - 1):

        @pl.when(ahead < chunks)
        def _():
            fetch(jnp.int32(ahead)).start()

    sums_ref[...] = jnp.zeros(sums_ref.shape, F32)

    def step(chunk, carry):
        @pl.when(chunk + RING - 1 < chunks)
        def _():
            fetch(chunk + RING - 1).start()

        fetch(chunk).wait()
        slot = lax.rem(chunk, RING)
        for at in range(CHUNK):
            k = chunk * CHUNK + at
            col = jnp.where(k < count, cols_ref[k], col_tiles)
            part = dot(received_ref[rows_ref[k]], buffer_ref[slot, at], 1, 0)
            sums_ref[col] += part
        return carry

    lax.fori_loop(0, chunks, step, 0)
    out_ref[...] = sums_ref[:col_tiles].astype(BF16)


def finish_kernel(parts_ref, feats_ref, weight_ref, second_ref, hidden_ref, send_ref):
    sources = parts_ref.shape[0]
    total = parts_ref[0].astype(F32)
    for source in range(1, sources):
        total = total + parts_ref[source].astype(F32)
    grad_hidden = jnp.concatenate(
        [total[tile].T for tile in range(total.shape[0])], axis=0
    ).astype(BF16)
    hidden_ref[...] = grad_hidden
    feats = feats_ref[...]
    pre = dot(feats, weight_ref[...], 1, 0)
    sig = sigmoid(pre)
    slope = sig * (1.0 + pre * (1.0 - sig))
    dpre = (grad_hidden.astype(F32) * slope).astype(BF16)
    first = dot(feats, dpre, 0, 0)
    features = first.shape[0]
    lanes = send_ref.shape[2]
    halves = features // lanes
    block = send_ref.shape[1]
    per_grad = features // block * halves
    for which, grad in enumerate((first, second_ref[...])):
        for half in range(halves):
            piece = grad[:, half * lanes : (half + 1) * lanes].astype(BF16)
            piece = piece.reshape(features // block, block, lanes)
            for row in range(features // block):
                send_ref[which * per_grad + row * halves + half] = piece[row]


def on_device(
    feats_one,
    feats_two,
    target_view,
    negatives,
    weight_one,
    weight_two,
    block_tiles,
    tile_rows,
    tile_cols,
    block_counts,
    need_rows,
):
    node_dev, features = feats_two.shape
    tile_size = block_tiles.shape[1]
    sources = lax.axis_size("col")
    row_group = lax.axis_size("row")
    devices = sources * row_group
    tiles_dev = node_dev // tile_size
    slot_count = need_rows.shape[2]
    col_count = row_group * tiles_dev
    row_slots = sources * slot_count
    weight_norm = 1.0 / math.sqrt(node_dev * devices)
    vmem = pl.BlockSpec(memory_space=pltpu.VMEM)
    smem = pl.BlockSpec(memory_space=pltpu.SMEM)

    wanted = lax.all_to_all(need_rows[0], "col", 0, 0, tiled=True)
    message, second = pl.pallas_call(
        message_kernel,
        out_shape=(
            jax.ShapeDtypeStruct((tiles_dev, features, tile_size), BF16),
            jax.ShapeDtypeStruct((features, features), F32),
        ),
        in_specs=[vmem] * 4,
        out_specs=(vmem, vmem),
        name="message",
    )(feats_two, target_view, negatives.reshape(1, node_dev), weight_two)
    send = pl.pallas_call(
        select_kernel,
        out_shape=jax.ShapeDtypeStruct((row_slots, features, tile_size), BF16),
        in_specs=[smem, vmem],
        out_specs=vmem,
        name="select",
    )(wanted, message)
    received = lax.all_to_all(
        send.reshape(sources, slot_count * features, tile_size), "col", 0, 0, tiled=True
    ).reshape(row_slots, features, tile_size)
    partial = pl.pallas_call(
        product_kernel,
        out_shape=jax.ShapeDtypeStruct((col_count, features, tile_size), BF16),
        in_specs=[smem, smem, smem, pl.BlockSpec(memory_space=pl.ANY), vmem],
        out_specs=vmem,
        scratch_shapes=[
            pltpu.VMEM((col_count + 1, features, tile_size), F32),
            pltpu.VMEM((RING, CHUNK, tile_size, tile_size), BF16),
            pltpu.SemaphoreType.DMA((RING,)),
        ],
        name="product",
    )(tile_rows, tile_cols, block_counts, block_tiles, received)
    parts = lax.all_to_all(
        partial.reshape(row_group, tiles_dev * features, tile_size), "row", 0, 0, tiled=True
    ).reshape(row_group, tiles_dev, features, tile_size)
    lanes = 128
    block = 2 * features * features // (devices * lanes)
    grad_hidden, grads = pl.pallas_call(
        finish_kernel,
        out_shape=(
            jax.ShapeDtypeStruct((node_dev, features), BF16),
            jax.ShapeDtypeStruct((devices, block, lanes), BF16),
        ),
        in_specs=[vmem] * 4,
        out_specs=(vmem, vmem),
        name="finish",
    )(parts, feats_one, weight_one, second)
    pieces = lax.all_to_all(grads, ("row", "col"), 0, 0, tiled=True)
    mine = jnp.sum(pieces.astype(F32), axis=0, keepdims=True) * weight_norm
    mine = mine.astype(BF16)
    whole = lax.all_to_all(
        jnp.broadcast_to(mine, (devices, block, lanes)), ("row", "col"), 0, 0, tiled=True
    )
    whole = whole.reshape(2, features // block, features // lanes, block, lanes)
    whole = whole.transpose(0, 1, 3, 2, 4).reshape(2, features, features).astype(F32)
    return (grad_hidden, whole[0], whole[1])


def solution(mesh):
    return jax.shard_map(
        on_device,
        mesh=mesh,
        in_specs=(
            P(("row", "col"), None),
            P(("row", "col"), None),
            P(("row", "col"), None),
            P(("row", "col")),
            P(),
            P(),
            P(("row", "col"), None, None),
            P(("row", "col")),
            P(("row", "col")),
            P(("row", "col")),
            P(("row", "col"), None, None),
        ),
        out_specs=(P(("row", "col"), None), P(), P()),
        check_vma=False,
    )
```
